32 devices in a mesh: blk: 4 (over z), hub: 4 (over y, x), rep: 2 (over core).
Axes of the slice: x: 2, y: 2, z: 4, core: 2. Of those that a mesh axis runs over, the one named last changes fastest.
Arguments:
- source_feats: bfloat16 [8192, 512], P(('blk', 'hub', 'rep')), may hold values from -6 to 6
- target_feats: bfloat16 [16384, 512], P(('blk', 'hub', 'rep')), may hold values from -6 to 6
- hub_feats: bfloat16 [512, 512], P(('blk', 'hub', 'rep')), may hold values from -6 to 6
- weight_self: bfloat16 [512, 256], replicated, may hold values from -0.25 to 0.25
- weight_neigh: bfloat16 [512, 256], replicated, may hold values from -0.25 to 0.25
- bias_vector: float32 [256], replicated, may hold values from -3 to 3
- send_rows: int32 [32, 4, 32], P(('blk', 'hub', 'rep')), may hold values from 0 to 255
- edge_target: int32 [32, 4096], P(('blk', 'hub', 'rep')), may hold values from 0 to 511
- edge_slot: int32 [32, 4096], P(('blk', 'hub', 'rep')), may hold values from 0 to 255, as said below
- hub_source: int32 [32, 512], P(('blk', 'hub', 'rep')), may hold values from 0 to 255
- hub_target: int32 [32, 512], P(('blk', 'hub', 'rep')), may hold values from 0 to 127
Outputs:
- vertex_out: bfloat16 [16384, 256], P(('blk', 'hub', 'rep'))
- hub_out: bfloat16 [512, 256], P(('blk', 'hub', 'rep'))
The draws below stay inside these ranges and needn't reach their ends.
Inputs may be any that keep to these rules, and one draw needn't show every extreme that they name: `edge_slot`: A value s < 128 names slot s of table_d (row s % 32 of the block that blk index s // 32 sends); larger values name hubs of the device's blk index. For each device and blk index the slots named lie within a prefix of that block, of uneven length.
All inputs are finite; a program needn't handle non-finite values.
Results may differ from the reference program's by a relative error of at most 0.0025.
Values may be sent and summed in bfloat16 or wider, within the bound.
No kernel may reach another device: no remote copies, remote signals or barrier semaphores. Data moves between devices by JAX's collectives and lax.ppermute only.
A program may use at most 64 MiB of HBM per device.

```python
import math
import jax
import jax.numpy as jnp
import numpy as np
from jax import lax

FEAT = 512
HIDDEN_SIZE = 256
CAP = 32
SRC_DEV = 256
DST_DEV = 512
E_DEV = 4096
EH_DEV = 512
G_HUB = 128
NSRC = 8192
NDST = 16384
NHUB = 512
N_BLK = 4
N_HUB = 4
N_REP = 2
DEVICES = 32


def draw_edge_slot(key, part):
    keys = jax.random.split(key, 6)
    lengths = jax.random.randint(keys[0], (DEVICES, N_BLK), 1, CAP + 1)
    longest = jax.random.randint(keys[1], (DEVICES, 1), 0, N_BLK)
    lengths = jnp.where(jnp.arange(N_BLK)[None, :] == longest, CAP, lengths)
    peer = jax.random.randint(keys[2], (DEVICES, E_DEV), 0, N_BLK)
    raw = jax.random.randint(keys[3], (DEVICES, E_DEV), 0, 1 << 20)
    within = raw % jnp.take_along_axis(lengths, peer, axis=1)
    hubpick = jax.random.randint(keys[4], (DEVICES, E_DEV), 0, G_HUB)
    chooser = jax.random.randint(keys[5], (DEVICES, E_DEV), 0, 8)
    return jnp.where(chooser == 0, N_BLK * CAP + hubpick, peer * CAP + within).astype(jnp.int32)


def with_ends(entries, key, smallest, largest):
    longest = entries.shape.index(max(entries.shape))
    spots = []
    for shift in (0, 1):
        where = [jax.random.randint(jax.random.fold_in(key, axis), (), 0, length) for axis, length in enumerate(entries.shape)]
        where[longest] = (where[longest] + shift) % entries.shape[longest]
        spots.append(tuple(where))
    return entries.at[spots[0]].set(smallest).at[spots[1]].set(largest)


def block_scale(rng, extent, cuts, least, top_value):
    loudness, own = 1.0, jax.random.fold_in(rng, 6)
    for axis_at, blocks in cuts:
        draws = jnp.exp(jax.random.uniform(jax.random.fold_in(own, axis_at), (blocks,), jnp.float32, least / len(cuts), top_value / len(cuts)))
        loudness = loudness * jnp.repeat(draws, extent[axis_at] // blocks).reshape([-1 if axis == axis_at else 1 for axis in range(len(extent))])
    return loudness


def cumulative_ranks(amount, lean):
    portions = [(1 << 20) // math.isqrt(standing ** lean) + 1 for standing in range(1, amount + 1)]
    width = 1 + sum(portions) // (1 << 30)
    return np.cumsum(np.array([max(1, weight // width) for weight in portions]))


def ranked_ids(stream_key, dims, number_of, lean):
    grid = cumulative_ranks(number_of, lean)
    pick = jax.random.randint(jax.random.fold_in(stream_key, 1), dims, 0, int(grid[number_of - 1]))
    grade = jnp.searchsorted(jnp.asarray(grid, jnp.int32), pick, side="right")
    return jax.random.permutation(jax.random.fold_in(stream_key, 2), number_of)[grade].astype(jnp.int32)


def scatter_about(rng, extent, scale, bound, pieces=(), held_as=jnp.bfloat16):
    array = jax.random.normal(rng, extent, jnp.float32) * scale
    if len(pieces) > 0:
        array = block_scale(rng, extent, pieces, -0.22, 0.18) * array
    return jnp.clip(array, min=-bound, max=bound).astype(held_as)


def setup_inputs(seed: int = 0) -> dict:
    splits = jax.random.split(jax.random.key(seed), 12)
    source_feats = scatter_about(splits[0], (NSRC, FEAT), 1.0, 6.0, ((0, 32),))
    target_feats = scatter_about(splits[1], (NDST, FEAT), 1.0, 6.0, ((0, 32),))
    hub_feats = scatter_about(splits[2], (NHUB, FEAT), 1.0, 6.0, ((0, 32),))
    weight_self = scatter_about(splits[3], (FEAT, HIDDEN_SIZE), FEAT ** -0.5, 0.25)
    weight_neigh = scatter_about(splits[4], (FEAT, HIDDEN_SIZE), FEAT ** -0.5, 0.25)
    bias_vector = scatter_about(splits[5], (HIDDEN_SIZE,), 0.5, 3.0, (), jnp.float32)
    send_rows = with_ends(jax.random.randint(splits[6], (DEVICES, N_BLK, CAP), 0, SRC_DEV), jax.random.fold_in(splits[6], 1), 0, SRC_DEV - 1).astype(jnp.int32)
    edge_target = with_ends(jax.random.randint(splits[7], (DEVICES, E_DEV), 0, DST_DEV), jax.random.fold_in(splits[7], 1), 0, DST_DEV - 1).astype(jnp.int32)
    edge_slot = draw_edge_slot(jax.random.fold_in(splits[11], 71), 0)
    hub_source = with_ends(jax.random.randint(splits[9], (DEVICES, EH_DEV), 0, SRC_DEV), jax.random.fold_in(splits[9], 1), 0, SRC_DEV - 1).astype(jnp.int32)
    hub_target = with_ends(ranked_ids(splits[10], (DEVICES, EH_DEV), G_HUB, 2), jax.random.fold_in(splits[10], 3), 0, G_HUB - 1).astype(jnp.int32)
    return dict(source_feats=source_feats, target_feats=target_feats, hub_feats=hub_feats, weight_self=weight_self, weight_neigh=weight_neigh, bias_vector=bias_vector, send_rows=send_rows, edge_target=edge_target, edge_slot=edge_slot, hub_source=hub_source, hub_target=hub_target)


def reference(source_feats, target_feats, hub_feats, weight_self, weight_neigh, bias_vector, send_rows, edge_target, edge_slot, hub_source, hub_target):
    groups = N_HUB * N_REP
    total = N_BLK * groups
    source_proj = jnp.dot(source_feats, weight_neigh, preferred_element_type=jnp.float32).astype(jnp.bfloat16)
    hub_proj = jnp.dot(hub_feats, weight_neigh, preferred_element_type=jnp.float32).astype(jnp.bfloat16)
    proj_grid = source_proj.reshape(N_BLK, groups, SRC_DEV, HIDDEN_SIZE)
    send_grid = send_rows.reshape(N_BLK, groups, N_BLK, CAP)
    peers = jnp.arange(N_BLK, dtype=jnp.int32)

    def per_device(device):
        blk_index = device // groups
        member = device % groups
        picked = send_grid[:, member, blk_index, :]
        arrived = proj_grid[peers[:, None], member, picked]
        hubs = lax.dynamic_slice_in_dim(hub_proj, (blk_index * G_HUB).astype(jnp.int32), G_HUB, 0)
        table = jnp.concatenate([arrived.reshape(N_BLK * CAP, HIDDEN_SIZE), hubs], axis=0)
        gathered = table[edge_slot[device]].astype(jnp.float32)
        neigh_sum = jax.ops.segment_sum(gathered, edge_target[device], DST_DEV)
        degree = jax.ops.segment_sum(jnp.ones((E_DEV,), jnp.float32), edge_target[device], DST_DEV)
        rows = lax.dynamic_slice_in_dim(target_feats, (device * DST_DEV).astype(jnp.int32), DST_DEV, 0)
        own = jnp.dot(rows, weight_self, preferred_element_type=jnp.float32)
        result = own + neigh_sum / jnp.maximum(degree, 1.0)[:, None] + bias_vector[None, :]
        return jnp.maximum(result, 0.0).astype(jnp.bfloat16)

    vertex_out = lax.map(per_device, jnp.arange(total, dtype=jnp.int32)).reshape(total * DST_DEV, HIDDEN_SIZE)
    src_grid = hub_source.reshape(N_BLK, groups, EH_DEV)
    dst_grid = hub_target.reshape(N_BLK, groups, EH_DEV)
    members = jnp.arange(groups, dtype=jnp.int32)

    def per_block(blk_index):
        rows = proj_grid[blk_index][members[:, None], src_grid[blk_index]]
        flat = rows.reshape(groups * EH_DEV, HIDDEN_SIZE).astype(jnp.float32)
        keys = dst_grid[blk_index].reshape(groups * EH_DEV)
        hub_sum = jax.ops.segment_sum(flat, keys, G_HUB)
        hub_degree = jax.ops.segment_sum(jnp.ones((groups * EH_DEV,), jnp.float32), keys, G_HUB)
        return hub_sum, hub_degree

    hub_sum, hub_degree = lax.map(per_block, jnp.arange(N_BLK, dtype=jnp.int32))
    hub_sum = hub_sum.reshape(N_BLK * G_HUB, HIDDEN_SIZE)
    hub_degree = hub_degree.reshape(N_BLK * G_HUB)
    own_hub = jnp.dot(hub_feats, weight_self, preferred_element_type=jnp.float32)
    hub_out = jnp.maximum(own_hub + hub_sum / jnp.maximum(hub_degree, 1.0)[:, None] + bias_vector[None, :], 0.0).astype(jnp.bfloat16)
    return vertex_out, hub_out
```

```python
import functools

import jax
import jax.numpy as jnp
from jax import lax
from jax.experimental import pallas as pl
from jax.experimental.pallas import tpu as pltpu
from jax.sharding import PartitionSpec as P

GROUP = ("hub", "rep")
F32 = jnp.float32
BF16 = jnp.bfloat16
COUNT_ROWS = 8


def bits_of(size):
    bits = size.bit_length() - 1
    assert size == 1 << bits
    return bits


def reverse_bits(value, bits):
    out = jnp.zeros_like(value)
    for i in range(bits):
        out = out | (((value >> i) & 1) << (bits - 1 - i))
    return out


def one_hot(ids, rows):
    lane = lax.broadcasted_iota(jnp.int32, (rows, ids.shape[1]), 0)
    return jnp.where(lane == ids, 1.0, 0.0).astype(BF16)


def dot_tn(a, b):
    return lax.dot_general(a, b, (((0,), (0,)), ((), ())), preferred_element_type=F32)


def dot_nt(a, b):
    return lax.dot_general(a, b, (((1,), (1,)), ((), ())), preferred_element_type=F32)


def project_kernel(
    members, peers, place, src, hub, w, send, h_src, h_tgt, out, keep, move, cnt, hubs
):
    proj = jnp.dot(src[...], w[...], preferred_element_type=F32).astype(BF16)
    hubs[...] = jnp.dot(hub[...], w[...], preferred_element_type=F32).astype(BF16).astype(F32)
    sources = src.shape[0]
    cap = send.shape[1]
    for k in range(peers):
        row = send[pl.ds(place[0] ^ k, 1), :]
        out[pl.ds(k * cap, cap), :] = dot_tn(one_hot(row, sources), proj).astype(BF16)
    picked = dot_tn(one_hot(h_src[...], sources), proj).astype(BF16)
    per = hub.shape[0]
    total = members * per
    shift = bits_of(per)
    target = h_tgt[...]
    owner = reverse_bits((target >> shift) ^ place[1], bits_of(members))
    slot = (owner << shift) | (target & (per - 1))
    partial = jnp.dot(one_hot(slot, total), picked, preferred_element_type=F32)
    keep[...] = partial[: total // 2]
    move[...] = partial[total // 2 :]
    width = w.shape[1]
    ones = jnp.ones((COUNT_ROWS, target.shape[1]), BF16)
    cnt[...] = dot_nt(ones, one_hot(target, width))


def count_kernel(peers, cap, place, tgt_feats, w, bias, e_tgt, e_slot, own, hi, lo, deg):
    own[...] = jnp.dot(tgt_feats[...], w[...], preferred_element_type=F32) + bias[...]
    targets, slots = hi.shape
    edges = e_tgt.shape[1]
    chunk = 512
    base = peers * cap
    raw = e_slot[...]
    slot = jnp.where(raw < base, raw ^ (place[0] * cap), base + ((raw - base) ^ place[2]))
    target = e_tgt[...]
    acc = jnp.zeros((targets, slots), F32)
    for c in range(0, edges, chunk):
        t = one_hot(target[:, c : c + chunk], targets)
        s = one_hot(slot[:, c : c + chunk], slots)
        acc = acc + dot_nt(t, s)
    top = jnp.floor(acc * (1.0 / 256.0))
    hi[...] = top.astype(BF16)
    lo[...] = (acc - 256.0 * top).astype(BF16)
    deg[...] = jnp.maximum(jnp.sum(acc, axis=1, keepdims=True), 1.0)


def finish_kernel(place, hi, lo, own, deg, table, hub, w, bias, sums, cnt, out, hub_out):
    rows = table[...]
    neigh = 256.0 * jnp.dot(hi[...], rows, preferred_element_type=F32) + jnp.dot(
        lo[...], rows, preferred_element_type=F32
    )
    out[...] = jnp.maximum(own[...] + neigh / deg[...], 0.0).astype(BF16)
    mine = jnp.dot(hub[...], w[...], preferred_element_type=F32) + bias[...]
    per = hub.shape[0]
    width = cnt.shape[1]
    r = lax.broadcasted_iota(jnp.int32, (per, width), 0)
    c = lax.broadcasted_iota(jnp.int32, (per, width), 1)
    degree = jnp.sum(
        jnp.where(c == r + place[1] * per, cnt[0:1, :], 0.0), axis=1, keepdims=True
    )
    hub_out[...] = jnp.maximum(mine + sums[...] / jnp.maximum(degree, 1.0), 0.0).astype(BF16)


def call(kernel, out_shape, *args):
    specs = [pl.BlockSpec(memory_space=pltpu.SMEM)]
    specs += [pl.BlockSpec(memory_space=pltpu.VMEM)] * (len(args) - 1)
    return pl.pallas_call(
        kernel,
        out_shape=out_shape,
        in_specs=specs,
        out_specs=jax.tree.map(lambda _: pl.BlockSpec(memory_space=pltpu.VMEM), out_shape),
    )(*args)


def swap(x, axes, size, bit):
    return lax.ppermute(x, axes, [(i, i ^ bit) for i in range(size)])


def on_device(
    source_feats,
    target_feats,
    hub_feats,
    weight_self,
    weight_neigh,
    bias_vector,
    send_rows,
    edge_target,
    edge_slot,
    hub_source,
    hub_target,
):
    shape = jax.ShapeDtypeStruct
    width = weight_neigh.shape[1]
    peers = lax.axis_size("blk")
    members = lax.axis_size(GROUP)
    cap = send_rows.shape[2]
    per = hub_feats.shape[0]
    group_hubs = members * per
    slots = peers * cap + group_hubs
    targets = target_feats.shape[0]
    bias = bias_vector[None, :]
    blk = lax.axis_index("blk")
    member = lax.axis_index(GROUP)
    place = jnp.stack([blk, member, member * per]).astype(jnp.int32)

    half = group_hubs // 2
    outgoing, keep, move, cnt, hubs = call(
        functools.partial(project_kernel, members, peers),
        (
            shape((peers * cap, width), BF16),
            shape((half, width), F32),
            shape((half, width), F32),
            shape((COUNT_ROWS, width), F32),
            shape((per, width), F32),
        ),
        place, source_feats, hub_feats, weight_neigh, send_rows[0], hub_source, hub_target,
    )
    own, hi, lo, deg = call(
        functools.partial(count_kernel, peers, cap),
        (
            shape((targets, width), F32),
            shape((targets, slots), BF16),
            shape((targets, slots), BF16),
            shape((targets, 1), F32),
        ),
        place, target_feats, weight_self, bias, edge_target, edge_slot,
    )

    for i in range(bits_of(members)):
        half = keep.shape[0]
        got = swap(jnp.concatenate([move, cnt, hubs], axis=0), GROUP, members, 1 << i)
        keep = keep + got[:half]
        cnt = cnt + got[half : half + COUNT_ROWS]
        hubs = jnp.concatenate([hubs, got[half + COUNT_ROWS :]], axis=0)
        if half > per:
            keep, move = keep[: half // 2], keep[half // 2 :]

    blocks = [outgoing[k * cap : (k + 1) * cap] for k in range(peers)]
    for i in range(bits_of(peers)):
        moved = [k for k in range(peers) if k >> i & 1]
        got = swap(jnp.concatenate([blocks[k] for k in moved], axis=0), "blk", peers, 1 << i)
        for j, k in enumerate(moved):
            blocks[k] = got[j * cap : (j + 1) * cap]

    table = jnp.concatenate(blocks + [hubs.astype(BF16)], axis=0)
    return call(
        finish_kernel,
        (shape((targets, width), BF16), shape((per, width), BF16)),
        place, hi, lo, own, deg, table, hub_feats, weight_self, bias, keep, cnt,
    )


def solution(mesh):
    split = P(("blk", "hub", "rep"))
    return jax.shard_map(
        on_device,
        mesh=mesh,
        in_specs=(split,) * 3 + (P(),) * 3 + (split,) * 5,
        out_specs=(split, split),
        check_vma=False,
    )
```

```python
import functools

import jax
import jax.numpy as jnp
from jax import lax
from jax.experimental import pallas as pl
from jax.experimental.pallas import tpu as pltpu
from jax.sharding import PartitionSpec as P

F32 = jnp.float32
BF16 = jnp.bfloat16
COUNT_ROWS = 16
BASE = 256


def bits_of(size):
    bits = size.bit_length() - 1
    assert size == 1 << bits
    return bits


def reverse_bits(value, bits):
    out = value & 0
    for i in range(bits):
        out = out | (((value >> i) & 1) << (bits - 1 - i))
    return out


def one_hot(ids, rows):
    row = lax.broadcasted_iota(jnp.int32, (rows, ids.shape[1]), 0)
    return jnp.where(row == ids, 1.0, 0.0).astype(BF16)


def dot_nn(a, b):
    return jnp.dot(a, b, preferred_element_type=F32)


def dot_nt(a, b):
    return lax.dot_general(a, b, (((1,), (1,)), ((), ())), preferred_element_type=F32)


def split_count(x):
    high = jnp.floor(x * (1.0 / BASE))
    return high.astype(BF16), (x - BASE * high).astype(BF16)


def split_sum(x):
    high = x.astype(BF16)
    return high, (x - high.astype(F32)).astype(BF16)


def places():
    return lax.axis_index("blk"), lax.axis_index("hub"), lax.axis_index("rep")


def pick(core, first, second):
    return jnp.where((core & 1) == 0, first, second)


def project_kernel(
    sizes, src_h, hub_h, w_h, send_h, hs_h, ht_h,
    out, message, keep, cnt,
    src, hub, w, send, hs, ht, lhs, sem,
):
    peers, n_hub, n_rep = sizes
    z, h, c = places()
    copies = [
        pltpu.make_async_copy(a, b, sem.at[i])
        for i, (a, b) in enumerate(
            ((send_h, send), (hs_h, hs), (ht_h, ht), (hub_h, hub), (src_h, src), (w_h, w))
        )
    ]
    for copy in copies:
        copy.start()
    sources = src.shape[0]
    cap = send.shape[2]
    per = hub.shape[0]
    width = w.shape[1]
    total = n_hub * n_rep * per
    half = total // 2
    for copy in copies[:3]:
        copy.wait()
    for p in range(peers):
        k = pick(c, p, reverse_bits(jnp.int32(p), bits_of(peers)))
        row = send[0, pl.ds(k ^ z, 1), :]
        lhs[:, p * cap : (p + 1) * cap] = one_hot(row, sources)
    target = ht[...]
    owner = target >> bits_of(per)
    other = owner & (n_rep - 1)
    x = (owner >> bits_of(n_rep)) ^ h
    order = jnp.where((other & 1) == 0, reverse_bits(x, bits_of(n_hub)), x)
    rep_part = reverse_bits(other ^ c, bits_of(n_rep))
    slot = (((rep_part << bits_of(n_hub)) | order) << bits_of(per)) | (target & (per - 1))
    picks = one_hot(hs[...], sources)
    high, low = split_count(dot_nt(picks, one_hot(slot, total)))
    base = peers * cap
    lhs[:, base : base + total] = low
    lhs[:, base + total :] = high
    ones = jnp.ones((8, target.shape[1]), BF16)
    counts = dot_nt(ones, one_hot(target, width))
    cnt[...] = counts
    high, low = split_count(counts)
    message[2 * half : 2 * half + COUNT_ROWS, :] = jnp.concatenate([high, low], axis=0)
    for copy in copies[3:]:
        copy.wait()
    proj = dot_nn(src[...], w[...]).astype(BF16)
    message[2 * half + COUNT_ROWS :, :] = dot_nn(hub[...], w[...]).astype(BF16)
    got = lax.dot_general(lhs[...], proj, (((0,), (0,)), ((), ())), preferred_element_type=F32)
    out[...] = got[:base].astype(BF16)
    sums = got[base : base + total] + BASE * got[base + total :]
    keep[...] = sums[:half]
    high, low = split_sum(sums[half:])
    message[:half, :] = high
    message[half : 2 * half, :] = low


def merge_kernel(got, sent, kept, cnt, *outs):
    n = kept.shape[0]
    sums = kept[...] + (got[:n].astype(F32) + got[n : 2 * n].astype(F32))
    count_at = 2 * n
    high = got[count_at : count_at + COUNT_ROWS].astype(F32)
    counts = cnt[...] + (BASE * high[:8] + high[8:])
    hubs_at = count_at + COUNT_ROWS
    if len(outs) == 2:
        keep, new_cnt = outs
        keep[...] = sums
        new_cnt[...] = counts
        return
    message, keep, new_cnt = outs
    half = n // 2
    keep[...] = sums[:half]
    new_cnt[...] = counts
    high, low = split_sum(sums[half:])
    message[:half, :] = high
    message[half : 2 * half, :] = low
    high, low = split_count(counts)
    message[2 * half : 2 * half + COUNT_ROWS, :] = jnp.concatenate([high, low], axis=0)
    rows = got.shape[0] - hubs_at
    new_at = 2 * half + COUNT_ROWS
    message[new_at : new_at + rows, :] = sent[hubs_at:, :]
    message[new_at + rows :, :] = got[hubs_at:, :]


def count_kernel(sizes, cap, per, tgt_feats, w, bias, e_tgt, e_slot, own, hi, lo, deg):
    peers, n_hub, n_rep = sizes
    z, h, c = places()
    own[...] = dot_nn(tgt_feats[...], w[...]) + bias[...]
    targets, slots = hi.shape
    edges = e_tgt.shape[1]
    chunk = 512
    base = peers * cap
    raw = e_slot[...]
    k = (raw >> bits_of(cap)) ^ z
    k = jnp.where((c & 1) == 0, k, reverse_bits(k, bits_of(peers)))
    low_slot = (k << bits_of(cap)) | (raw & (cap - 1))
    hub = raw - base
    owner = hub >> bits_of(per)
    x = (owner >> bits_of(n_rep)) ^ h
    x = jnp.where((c & 1) == 0, x, reverse_bits(x, bits_of(n_hub)))
    q = (x << bits_of(n_rep)) | ((owner & (n_rep - 1)) ^ c)
    hub_slot = base + ((q << bits_of(per)) | (hub & (per - 1)))
    slot = jnp.where(raw < base, low_slot, hub_slot)
    target = e_tgt[...]
    acc = jnp.zeros((targets, slots), F32)
    for s in range(0, edges, chunk):
        acc = acc + dot_nt(
            one_hot(target[:, s : s + chunk], targets), one_hot(slot[:, s : s + chunk], slots)
        )
    hi[...], lo[...] = split_count(acc)
    deg[...] = jnp.maximum(jnp.sum(acc, axis=1, keepdims=True), 1.0)


def finish_kernel(
    sizes, hi, lo, own, deg, rows, got, sent, kept, cnt, hub, w, bias, out, hub_out, table
):
    peers, n_hub, n_rep = sizes
    z, h, c = places()
    per = hub.shape[0]
    base = rows.shape[0]
    hubs_at = 2 * per + COUNT_ROWS
    n = got.shape[0] - hubs_at
    table[:base, :] = rows[...]
    table[base : base + n, :] = sent[hubs_at:, :]
    table[base + n :, :] = got[hubs_at:, :]
    values = table[...]
    neigh = BASE * dot_nn(hi[...], values) + dot_nn(lo[...], values)
    out[...] = jnp.maximum(own[...] + neigh / deg[...], 0.0).astype(BF16)
    mine = dot_nn(hub[...], w[...]) + bias[...]
    sums = kept[...] + (got[:per].astype(F32) + got[per : 2 * per].astype(F32))
    high = got[2 * per : 2 * per + COUNT_ROWS].astype(F32)
    counts = cnt[...] + (BASE * high[:8] + high[8:])
    width = cnt.shape[1]
    row = lax.broadcasted_iota(jnp.int32, (per, width), 0)
    lane = lax.broadcasted_iota(jnp.int32, (per, width), 1)
    first = (h * n_rep + c) * per
    degree = jnp.sum(jnp.where(lane == row + first, counts[0:1, :], 0.0), axis=1, keepdims=True)
    hub_out[...] = jnp.maximum(mine + sums / jnp.maximum(degree, 1.0), 0.0).astype(BF16)


def call(name, kernel, out_shape, *args, mib=8, hbm=False, scratch=()):
    spec = pl.BlockSpec(memory_space=pltpu.HBM if hbm else pltpu.VMEM)
    if hbm:
        args = [pltpu.with_memory_space_constraint(a, pltpu.HBM) for a in args]
    with jax.named_scope(name):
        return pl.pallas_call(
            kernel,
            out_shape=out_shape,
            in_specs=[spec] * len(args),
            out_specs=jax.tree.map(lambda _: pl.BlockSpec(memory_space=pltpu.VMEM), out_shape),
            scratch_shapes=scratch,
            compiler_params=pltpu.CompilerParams(vmem_limit_bytes=mib << 20),
            name=name,
        )(*args)


def swap(name, x, axis, size, n_rep, step):
    last = bits_of(size) - 1
    pairs = []
    for i in range(size):
        for c in range(n_rep):
            bit = step if c % 2 == 0 else last - step
            pairs.append((i * n_rep + c, (i ^ (1 << bit)) * n_rep + c))
    with jax.named_scope(name):
        return lax.ppermute(x, (axis, "rep"), pairs)


def on_device(
    source_feats,
    target_feats,
    hub_feats,
    weight_self,
    weight_neigh,
    bias_vector,
    send_rows,
    edge_target,
    edge_slot,
    hub_source,
    hub_target,
):
    shape = jax.ShapeDtypeStruct
    width = weight_neigh.shape[1]
    sizes = tuple(lax.axis_size(a) for a in ("blk", "hub", "rep"))
    peers, n_hub, n_rep = sizes
    assert n_rep == 2
    cap = send_rows.shape[2]
    per = hub_feats.shape[0]
    group_hubs = n_hub * n_rep * per
    assert group_hubs <= width
    slots = peers * cap + group_hubs
    targets = target_feats.shape[0]
    bias = bias_vector[None, :]

    half = group_hubs // 2
    first = [send_rows, hub_source, hub_target, hub_feats, source_feats, weight_neigh]
    outgoing, message, keep, cnt = call(
        "project",
        functools.partial(project_kernel, sizes),
        (
            shape((peers * cap, width), BF16),
            shape((2 * half + COUNT_ROWS + per, width), BF16),
            shape((half, width), F32),
            shape((8, width), F32),
        ),
        source_feats, hub_feats, weight_neigh, send_rows, hub_source, hub_target,
        hbm=True,
        scratch=[
            pltpu.VMEM(a.shape, a.dtype)
            for a in (source_feats, hub_feats, weight_neigh, send_rows, hub_source, hub_target)
        ]
        + [
            pltpu.VMEM((source_feats.shape[0], peers * cap + 2 * group_hubs), BF16),
            pltpu.SemaphoreType.DMA((len(first),)),
        ],
    )

    with jax.named_scope("h0"):
        got = lax.ppermute(message, "rep", [(i, i ^ 1) for i in range(n_rep)])
    for i in range(bits_of(n_hub)):
        half = keep.shape[0] // 2
        rows = got.shape[0] - 2 * keep.shape[0] - COUNT_ROWS
        message, keep, cnt = call(
            f"merge{i}",
            merge_kernel,
            (
                shape((2 * half + COUNT_ROWS + 2 * rows, width), BF16),
                shape((half, width), F32),
                shape((8, width), F32),
            ),
            got, message, keep, cnt,
        )
        got = swap(f"h{i + 1}", message, "hub", n_hub, n_rep, i)

    blocks = [outgoing[k * cap : (k + 1) * cap] for k in range(peers)]
    for i in range(bits_of(peers)):
        moved = [k for k in range(peers) if k >> i & 1]
        arrived = swap(
            f"z{i}", jnp.concatenate([blocks[k] for k in moved], axis=0), "blk", peers, n_rep, i
        )
        for j, k in enumerate(moved):
            blocks[k] = arrived[j * cap : (j + 1) * cap]

    own, hi, lo, deg = call(
        "count",
        functools.partial(count_kernel, sizes, cap, per),
        (
            shape((targets, width), F32),
            shape((targets, slots), BF16),
            shape((targets, slots), BF16),
            shape((targets, 1), F32),
        ),
        target_feats, weight_self, bias, edge_target, edge_slot, mib=24,
    )
    return call(
        "finish",
        functools.partial(finish_kernel, sizes),
        (shape((targets, width), BF16), shape((per, width), BF16)),
        hi, lo, own, deg, jnp.concatenate(blocks, axis=0), got, message, keep, cnt,
        hub_feats, weight_self, bias,
        mib=24 if slots > 1024 else 8,
        scratch=[pltpu.VMEM((slots, width), BF16)],
    )


def solution(mesh):
    split = P(("blk", "hub", "rep"))
    return jax.shard_map(
        on_device,
        mesh=mesh,
        in_specs=(split,) * 3 + (P(),) * 3 + (split,) * 5,
        out_specs=(split, split),
        check_vma=False,
    )
```

```python
import functools

import jax
import jax.numpy as jnp
from jax import lax
from jax.experimental import pallas as pl
from jax.experimental.pallas import tpu as pltpu
from jax.sharding import PartitionSpec as P


F32 = jnp.float32
BF16 = jnp.bfloat16
COUNT_ROWS = 16
BASE = 256


def bits_of(size):
    bits = size.bit_length() - 1
    assert size == 1 << bits
    return bits


def reverse_bits(value, bits):
    out = value & 0
    for i in range(bits):
        out = out | (((value >> i) & 1) << (bits - 1 - i))
    return out


def one_hot(ids, rows):
    row = lax.broadcasted_iota(jnp.int32, (rows, ids.shape[1]), 0)
    return jnp.where(row == ids, 1.0, 0.0).astype(BF16)


def dot_nn(a, b):
    return jnp.dot(a, b, preferred_element_type=F32)


def dot_nt(a, b):
    return lax.dot_general(a, b, (((1,), (1,)), ((), ())), preferred_element_type=F32)


def split_count(x):
    high = jnp.floor(x * (1.0 / BASE))
    return high.astype(BF16), (x - BASE * high).astype(BF16)


def split_sum(x):
    high = x.astype(BF16)
    return high, (x - high.astype(F32)).astype(BF16)


def parity(value, bits):
    out = value & 1
    for i in range(1, bits):
        out = out ^ ((value >> i) & 1)
    return out


def places(n_hub):
    z, h, c = lax.axis_index("blk"), lax.axis_index("hub"), lax.axis_index("rep")
    return z, h, c, c ^ parity(h, bits_of(n_hub))


def pick(core, first, second):
    return jnp.where((core & 1) == 0, first, second)


def project_kernel(
    sizes, src_h, hub_h, w_h, send_h, hs_h, ht_h, et_h, es_h, bias_h,
    out, message, keep, cnt, et, es, bias, hub,
    src, w, send, hs, ht, lhs, sem,
):
    peers, n_hub, n_rep = sizes
    z, h, c, side = places(n_hub)
    copies = [
        pltpu.make_async_copy(a, b, sem.at[i])
        for i, (a, b) in enumerate(
            (
                (send_h, send), (hs_h, hs), (ht_h, ht),
                (hub_h, hub), (src_h, src), (w_h, w), (et_h, et), (es_h, es),
                (bias_h, bias),
            )
        )
    ]
    for copy in copies:
        copy.start()
    sources = src.shape[0]
    cap = send.shape[2]
    per = hub.shape[0]
    width = w.shape[1]
    total = n_hub * n_rep * per
    half = total // 2
    for copy in copies[:3]:
        copy.wait()
    for p in range(peers):
        k = pick(c, p, reverse_bits(jnp.int32(p), bits_of(peers)))
        row = send[0, pl.ds(k ^ z, 1), :]
        lhs[:, p * cap : (p + 1) * cap] = one_hot(row, sources)
    target = ht[...]
    owner = target >> bits_of(per)
    chip = owner >> 1
    other = (owner & 1) ^ parity(chip, bits_of(n_hub))
    x = chip ^ h
    order = jnp.where(other == 0, reverse_bits(x, bits_of(n_hub)), x)
    order = order | ((other ^ side) << bits_of(n_hub))
    slot = (order << bits_of(per)) | (target & (per - 1))
    picks = one_hot(hs[...], sources)
    high, low = split_count(dot_nt(picks, one_hot(slot, total)))
    base = peers * cap
    lhs[:, base : base + total] = low
    lhs[:, base + total :] = high
    ones = jnp.ones((8, target.shape[1]), BF16)
    counts = dot_nt(ones, one_hot(target, width))
    cnt[...] = counts
    high, low = split_count(counts)
    message[2 * half : 2 * half + COUNT_ROWS, :] = jnp.concatenate([high, low], axis=0)
    for copy in copies[3:6]:
        copy.wait()
    proj = dot_nn(src[...], w[...]).astype(BF16)
    message[2 * half + COUNT_ROWS :, :] = dot_nn(hub[...], w[...]).astype(BF16)
    got = lax.dot_general(lhs[...], proj, (((0,), (0,)), ((), ())), preferred_element_type=F32)
    out[...] = got[:base].astype(BF16)
    sums = got[base : base + total] + BASE * got[base + total :]
    keep[...] = sums[:half]
    high, low = split_sum(sums[half:])
    message[:half, :] = high
    message[half : 2 * half, :] = low
    for copy in copies[6:]:
        copy.wait()


def merge_kernel(got, sent, kept, cnt, *outs):
    n = kept.shape[0]
    sums = kept[...] + (got[:n].astype(F32) + got[n : 2 * n].astype(F32))
    count_at = 2 * n
    high = got[count_at : count_at + COUNT_ROWS].astype(F32)
    counts = cnt[...] + (BASE * high[:8] + high[8:])
    hubs_at = count_at + COUNT_ROWS
    if len(outs) == 2:
        keep, new_cnt = outs
        keep[...] = sums
        new_cnt[...] = counts
        return
    message, keep, new_cnt = outs
    half = n // 2
    keep[...] = sums[:half]
    new_cnt[...] = counts
    high, low = split_sum(sums[half:])
    message[:half, :] = high
    message[half : 2 * half, :] = low
    high, low = split_count(counts)
    message[2 * half : 2 * half + COUNT_ROWS, :] = jnp.concatenate([high, low], axis=0)
    rows = got.shape[0] - hubs_at
    new_at = 2 * half + COUNT_ROWS
    message[new_at : new_at + rows, :] = sent[hubs_at:, :]
    message[new_at + rows :, :] = got[hubs_at:, :]


def edge_slots(sizes, cap, per, raw):
    peers, n_hub, _ = sizes
    z, h, c, side = places(n_hub)
    base = peers * cap
    k = (raw >> bits_of(cap)) ^ z
    k = jnp.where((c & 1) == 0, k, reverse_bits(k, bits_of(peers)))
    low_slot = (k << bits_of(cap)) | (raw & (cap - 1))
    hub = raw - base
    owner = hub >> bits_of(per)
    chip = owner >> 1
    x = chip ^ h
    x = jnp.where(side == 0, x, reverse_bits(x, bits_of(n_hub)))
    q = (x << 1) | ((owner & 1) ^ parity(chip, bits_of(n_hub)) ^ side)
    hub_slot = base + ((q << bits_of(per)) | (hub & (per - 1)))
    return jnp.where(raw < base, low_slot, hub_slot)


def edge_counts(targets, slots, target, slot, first, last):
    chunk = 512
    acc = jnp.zeros((targets, slots), F32)
    for s in range(first, last, chunk):
        acc = acc + dot_nt(
            one_hot(target[:, s : s + chunk], targets), one_hot(slot[:, s : s + chunk], slots)
        )
    return acc


def own_kernel(sizes, cap, per, tgt_feats, w, bias, e_tgt, e_slot, own, acc):
    own[...] = dot_nn(tgt_feats[...], w[...]) + bias[...]
    slot = edge_slots(sizes, cap, per, e_slot[...])
    acc[...] = edge_counts(*acc.shape, e_tgt[...], slot, 0, e_slot.shape[1] // 2)


def count_kernel(sizes, cap, per, acc, e_tgt, e_slot, hi, lo, deg):
    slot = edge_slots(sizes, cap, per, e_slot[...])
    edges = e_slot.shape[1]
    counts = acc[...] + edge_counts(*acc.shape, e_tgt[...], slot, edges // 2, edges)
    hi[...], lo[...] = split_count(counts)
    deg[...] = jnp.maximum(jnp.sum(counts, axis=1, keepdims=True), 1.0)


def finish_kernel(
    sizes, hi, lo, own, deg, rows, got, sent, kept, cnt, hub, w, bias, out, hub_out, table
):
    _, n_hub, n_rep = sizes
    _, h, c, _ = places(n_hub)
    per = hub.shape[0]
    base = rows.shape[0]
    hubs_at = 2 * per + COUNT_ROWS
    n = got.shape[0] - hubs_at
    table[:base, :] = rows[...]
    table[base : base + n, :] = sent[hubs_at:, :]
    table[base + n :, :] = got[hubs_at:, :]
    values = table[...]
    neigh = BASE * dot_nn(hi[...], values) + dot_nn(lo[...], values)
    out[...] = jnp.maximum(own[...] + neigh / deg[...], 0.0).astype(BF16)
    mine = dot_nn(hub[...], w[...]) + bias[...]
    sums = kept[...] + (got[:per].astype(F32) + got[per : 2 * per].astype(F32))
    high = got[2 * per : 2 * per + COUNT_ROWS].astype(F32)
    counts = cnt[...] + (BASE * high[:8] + high[8:])
    width = cnt.shape[1]
    row = lax.broadcasted_iota(jnp.int32, (per, width), 0)
    lane = lax.broadcasted_iota(jnp.int32, (per, width), 1)
    first = (h * n_rep + c) * per
    degree = jnp.sum(jnp.where(lane == row + first, counts[0:1, :], 0.0), axis=1, keepdims=True)
    hub_out[...] = jnp.maximum(mine + sums / jnp.maximum(degree, 1.0), 0.0).astype(BF16)


def call(kernel, out_shape, *args, mib=8, hbm=False, scratch=()):
    spec = pl.BlockSpec(memory_space=pltpu.HBM if hbm else pltpu.VMEM)
    if hbm:
        args = [pltpu.with_memory_space_constraint(a, pltpu.HBM) for a in args]
    return pl.pallas_call(
        kernel,
        out_shape=out_shape,
        in_specs=[spec] * len(args),
        out_specs=jax.tree.map(lambda _: pl.BlockSpec(memory_space=pltpu.VMEM), out_shape),
        scratch_shapes=scratch,
        compiler_params=pltpu.CompilerParams(vmem_limit_bytes=mib << 20),
    )(*args)


def swap_hub(x, n_hub, step):
    bits = bits_of(n_hub)
    pairs = []
    for h in range(n_hub):
        for side in range(2):
            to = h ^ (1 << (step if side == 0 else bits - 1 - step))
            pairs.append((2 * h + (side ^ parity(h, bits)), 2 * to + (side ^ parity(to, bits))))
    return lax.ppermute(x, ("hub", "rep"), pairs)


def swap_blk(x, peers, step):
    pairs = []
    for z in range(peers):
        for c in range(2):
            to = z ^ (1 << (step if c == 0 else bits_of(peers) - 1 - step))
            pairs.append((2 * z + c, 2 * to + c))
    return lax.ppermute(x, ("blk", "rep"), pairs)


def on_device(
    source_feats,
    target_feats,
    hub_feats,
    weight_self,
    weight_neigh,
    bias_vector,
    send_rows,
    edge_target,
    edge_slot,
    hub_source,
    hub_target,
):
    shape = jax.ShapeDtypeStruct
    width = weight_neigh.shape[1]
    sizes = tuple(lax.axis_size(a) for a in ("blk", "hub", "rep"))
    peers, n_hub, n_rep = sizes
    assert n_rep == 2
    cap = send_rows.shape[2]
    per = hub_feats.shape[0]
    group_hubs = n_hub * n_rep * per
    assert group_hubs <= width
    slots = peers * cap + group_hubs
    targets = target_feats.shape[0]
    bias = bias_vector[None, :]

    half = group_hubs // 2
    outgoing, message, keep, cnt, e_tgt, e_slot, bias, hubs = call(
        functools.partial(project_kernel, sizes),
        (
            shape((peers * cap, width), BF16),
            shape((2 * half + COUNT_ROWS + per, width), BF16),
            shape((half, width), F32),
            shape((8, width), F32),
            shape(edge_target.shape, jnp.int32),
            shape(edge_slot.shape, jnp.int32),
            shape(bias.shape, F32),
            shape(hub_feats.shape, BF16),
        ),
        source_feats, hub_feats, weight_neigh, send_rows, hub_source, hub_target,
        edge_target, edge_slot, bias,
        hbm=True,
        scratch=[
            pltpu.VMEM(a.shape, a.dtype)
            for a in (source_feats, weight_neigh, send_rows, hub_source, hub_target)
        ]
        + [
            pltpu.VMEM((source_feats.shape[0], peers * cap + 2 * group_hubs), BF16),
            pltpu.SemaphoreType.DMA((9,)),
        ],
    )

    got = lax.ppermute(message, "rep", [(i, i ^ 1) for i in range(n_rep)])
    for i in range(bits_of(n_hub)):
        half = keep.shape[0] // 2
        rows = got.shape[0] - 2 * keep.shape[0] - COUNT_ROWS
        message, keep, cnt = call(
            merge_kernel,
            (
                shape((2 * half + COUNT_ROWS + 2 * rows, width), BF16),
                shape((half, width), F32),
                shape((8, width), F32),
            ),
            got, message, keep, cnt,
        )
        got = swap_hub(message, n_hub, i)

    blocks = [outgoing[k * cap : (k + 1) * cap] for k in range(peers)]
    for i in range(bits_of(peers)):
        moved = [k for k in range(peers) if k >> i & 1]
        arrived = swap_blk(jnp.concatenate([blocks[k] for k in moved], axis=0), peers, i)
        for j, k in enumerate(moved):
            blocks[k] = arrived[j * cap : (j + 1) * cap]

    own, acc = call(
        functools.partial(own_kernel, sizes, cap, per),
        (shape((targets, width), F32), shape((targets, slots), F32)),
        target_feats, weight_self, bias, e_tgt, e_slot, mib=24,
    )
    hi, lo, deg = call(
        functools.partial(count_kernel, sizes, cap, per),
        (
            shape((targets, slots), BF16),
            shape((targets, slots), BF16),
            shape((targets, 1), F32),
        ),
        acc, e_tgt, e_slot, mib=24,
    )
    return call(
        functools.partial(finish_kernel, sizes),
        (shape((targets, width), BF16), shape((per, width), BF16)),
        hi, lo, own, deg, jnp.concatenate(blocks, axis=0), got, message, keep, cnt,
        hubs, weight_self, bias,
        mib=24 if slots > 1024 else 8,
        scratch=[pltpu.VMEM((slots, width), BF16)],
    )


def solution(mesh):
    split = P(("blk", "hub", "rep"))

    return jax.shard_map(
        on_device,
        mesh=mesh,
        in_specs=(split,) * 3 + (P(),) * 3 + (split,) * 5,
        out_specs=(split, split),
        check_vma=False,
    )
```

```python
import functools

import jax
import jax.numpy as jnp
from jax import lax
from jax.experimental import pallas as pl
from jax.experimental.pallas import tpu as pltpu
from jax.sharding import PartitionSpec as P


F32 = jnp.float32
BF16 = jnp.bfloat16
COUNT_ROWS = 16
BASE = 256


def bits_of(size):
    bits = size.bit_length() - 1
    assert size == 1 << bits
    return bits


def reverse_bits(value, bits):
    out = value & 0
    for i in range(bits):
        out = out | (((value >> i) & 1) << (bits - 1 - i))
    return out


def one_hot(ids, rows):
    row = lax.broadcasted_iota(jnp.int32, (rows, ids.shape[1]), 0)
    return jnp.where(row == ids, 1.0, 0.0).astype(BF16)


def dot_nn(a, b):
    return jnp.dot(a, b, preferred_element_type=F32)


def dot_nt(a, b):
    return lax.dot_general(a, b, (((1,), (1,)), ((), ())), preferred_element_type=F32)


def split_count(x):
    high = jnp.floor(x * (1.0 / BASE))
    return high.astype(BF16), (x - BASE * high).astype(BF16)


def split_sum(x):
    high = x.astype(BF16)
    return high, (x - high.astype(F32)).astype(BF16)


def parity(value, bits):
    out = value & 1
    for i in range(1, bits):
        out = out ^ ((value >> i) & 1)
    return out


def places(n_hub):
    z, h, c = lax.axis_index("blk"), lax.axis_index("hub"), lax.axis_index("rep")
    return z, h, c, c ^ parity(h, bits_of(n_hub))


def project_kernel(
    sizes, src_h, hub_h, w_h, send_h, hs_h, ht_h, et_h, es_h, bias_h, tgt_h, ws_h,
    out, message, keep, cnt, et, es, bias, hub, tgt, ws,
    src, w, send, hs, ht, lhs, sem,
):
    peers, n_hub, n_rep = sizes
    z, h, c, side = places(n_hub)
    copies = [
        pltpu.make_async_copy(a, b, sem.at[i])
        for i, (a, b) in enumerate(
            (
                (send_h, send), (hs_h, hs), (ht_h, ht),
                (src_h, src), (w_h, w), (hub_h, hub), (et_h, et), (es_h, es),
                (bias_h, bias), (ws_h, ws), (tgt_h, tgt),
            )
        )
    ]
    for copy in copies:
        copy.start()
    sources = src.shape[0]
    cap = send.shape[2]
    per = hub.shape[0]
    width = w.shape[1]
    total = n_hub * n_rep * per
    half = total // 2
    for copy in copies[:3]:
        copy.wait()
    for p in range(peers):
        k = jnp.where((c & 1) == 1, p, reverse_bits(jnp.int32(p), bits_of(peers)))
        row = send[0, pl.ds(k ^ z, 1), :]
        lhs[p * cap : (p + 1) * cap, :] = one_hot(row, sources).T
    target = ht[...]
    owner = target >> bits_of(per)
    chip = owner >> 1
    other = (owner & 1) ^ parity(chip, bits_of(n_hub))
    x = chip ^ h
    order = jnp.where(other == 1, reverse_bits(x, bits_of(n_hub)), x)
    order = order | ((other ^ side) << bits_of(n_hub))
    slot = (order << bits_of(per)) | (target & (per - 1))
    picks = one_hot(hs[...], sources)
    high, low = split_count(dot_nt(one_hot(slot, total), picks))
    base = peers * cap
    lhs[base : base + total, :] = low
    lhs[base + total :, :] = high
    ones = jnp.ones((8, target.shape[1]), BF16)
    counts = dot_nt(ones, one_hot(target, width))
    cnt[...] = counts
    high, low = split_count(counts)
    message[2 * half : 2 * half + COUNT_ROWS, :] = jnp.concatenate([high, low], axis=0)
    for copy in copies[3:6]:
        copy.wait()
    proj = dot_nn(src[...], w[...]).astype(BF16)
    message[2 * half + COUNT_ROWS :, :] = dot_nn(hub[...], w[...]).astype(BF16)
    got = dot_nn(lhs[...], proj)
    out[...] = got[:base].astype(BF16)
    sums = got[base : base + total] + BASE * got[base + total :]
    keep[...] = sums[:half]
    high, low = split_sum(sums[half:])
    message[:half, :] = high
    message[half : 2 * half, :] = low
    for copy in copies[6:]:
        copy.wait()


def merge_kernel(got, sent, kept, cnt, *outs):
    n = kept.shape[0]
    sums = kept[...] + (got[:n].astype(F32) + got[n : 2 * n].astype(F32))
    count_at = 2 * n
    high = got[count_at : count_at + COUNT_ROWS].astype(F32)
    counts = cnt[...] + (BASE * high[:8] + high[8:])
    hubs_at = count_at + COUNT_ROWS
    if len(outs) == 2:
        keep, new_cnt = outs
        keep[...] = sums
        new_cnt[...] = counts
        return
    message, keep, new_cnt = outs
    half = n // 2
    keep[...] = sums[:half]
    new_cnt[...] = counts
    high, low = split_sum(sums[half:])
    message[:half, :] = high
    message[half : 2 * half, :] = low
    high, low = split_count(counts)
    message[2 * half : 2 * half + COUNT_ROWS, :] = jnp.concatenate([high, low], axis=0)
    rows = got.shape[0] - hubs_at
    new_at = 2 * half + COUNT_ROWS
    message[new_at : new_at + rows, :] = sent[hubs_at:, :]
    message[new_at + rows :, :] = got[hubs_at:, :]


def edge_slots(sizes, cap, per, raw):
    peers, n_hub, _ = sizes
    z, h, c, side = places(n_hub)
    base = peers * cap
    k = (raw >> bits_of(cap)) ^ z
    k = jnp.where((c & 1) == 1, k, reverse_bits(k, bits_of(peers)))
    low_slot = (k << bits_of(cap)) | (raw & (cap - 1))
    hub = raw - base
    owner = hub >> bits_of(per)
    chip = owner >> 1
    x = chip ^ h
    x = jnp.where(side == 1, x, reverse_bits(x, bits_of(n_hub)))
    q = (x << 1) | ((owner & 1) ^ parity(chip, bits_of(n_hub)) ^ side)
    hub_slot = base + ((q << bits_of(per)) | (hub & (per - 1)))
    return jnp.where(raw < base, low_slot, hub_slot)


def edge_counts(targets, slots, target, slot, first, last):
    chunk = 512
    acc = jnp.zeros((targets, slots), F32)
    for s in range(first, last, chunk):
        acc = acc + dot_nt(
            one_hot(target[:, s : s + chunk], targets), one_hot(slot[:, s : s + chunk], slots)
        )
    return acc


def own_kernel(sizes, cap, per, tgt_feats, w, bias, e_tgt, e_slot, own, acc):
    own[...] = dot_nn(tgt_feats[...], w[...]) + bias[...]
    slot = edge_slots(sizes, cap, per, e_slot[...])
    acc[...] = edge_counts(*acc.shape, e_tgt[...], slot, 0, e_slot.shape[1] // 2)


def count_kernel(sizes, cap, per, acc, e_tgt, e_slot, hi, lo, late, scale):
    slot = edge_slots(sizes, cap, per, e_slot[...])
    edges = e_slot.shape[1]
    counts = acc[...] + edge_counts(*acc.shape, e_tgt[...], slot, edges // 2, edges)
    early = hi.shape[1]
    high = jnp.floor(counts * (1.0 / BASE))
    low = counts - BASE * high
    hi[...] = high[:, :early].astype(BF16)
    lo[...] = low[:, :early].astype(BF16)
    span = late.shape[1]
    lane = lax.broadcasted_iota(jnp.int32, late.shape, 1)
    moved = pltpu.roll(low[:, -span:], span // 2, 1)
    late[...] = jnp.where(lane < span // 2, moved, high[:, -span:]).astype(BF16)
    degree = jnp.maximum(jnp.sum(counts, axis=1, keepdims=True), 1.0)
    scale[...] = jnp.broadcast_to(1.0 / degree, scale.shape)


def blend_kernel(hi, lo, own, scale, rows, sent, hub, w, bias, mean, mine, table):
    base = rows.shape[0]
    table[:base, :] = rows[...]
    table[base:, :] = sent[sent.shape[0] - (table.shape[0] - base) :, :]
    values = table[...]
    neigh = BASE * dot_nn(hi[...], values) + dot_nn(lo[...], values)
    mean[...] = own[...] + neigh * scale[...]
    mine[...] = dot_nn(hub[...], w[...]) + bias[...]


def finish_kernel(sizes, mean, late, scale, got, kept, cnt, mine, out, hub_out):
    _, n_hub, n_rep = sizes
    _, h, c, _ = places(n_hub)
    per = mine.shape[0]
    hubs_at = 2 * per + COUNT_ROWS
    rows = got[hubs_at:, :]
    values = jnp.concatenate([rows, (BASE * rows.astype(F32)).astype(BF16)], axis=0)
    neigh = dot_nn(late[...], values)
    out[...] = jnp.maximum(mean[...] + neigh * scale[...], 0.0).astype(BF16)
    sums = kept[...] + (got[:per].astype(F32) + got[per : 2 * per].astype(F32))
    high = got[2 * per : 2 * per + COUNT_ROWS].astype(F32)
    counts = cnt[...] + (BASE * high[:8] + high[8:])
    width = cnt.shape[1]
    row = lax.broadcasted_iota(jnp.int32, (per, width), 0)
    lane = lax.broadcasted_iota(jnp.int32, (per, width), 1)
    first = (h * n_rep + c) * per
    degree = jnp.sum(jnp.where(lane == row + first, counts[0:1, :], 0.0), axis=1, keepdims=True)
    hub_out[...] = jnp.maximum(mine[...] + sums / jnp.maximum(degree, 1.0), 0.0).astype(BF16)


def call(kernel, out_shape, *args, mib=8, hbm=False, scratch=()):
    spec = pl.BlockSpec(memory_space=pltpu.HBM if hbm else pltpu.VMEM)
    if hbm:
        args = [pltpu.with_memory_space_constraint(a, pltpu.HBM) for a in args]
    return pl.pallas_call(
        kernel,
        out_shape=out_shape,
        in_specs=[spec] * len(args),
        out_specs=jax.tree.map(lambda _: pl.BlockSpec(memory_space=pltpu.VMEM), out_shape),
        scratch_shapes=scratch,
        compiler_params=pltpu.CompilerParams(vmem_limit_bytes=mib << 20),
    )(*args)


def swap_hub(x, n_hub, step):
    bits = bits_of(n_hub)
    pairs = []
    for h in range(n_hub):
        for side in range(2):
            to = h ^ (1 << (step if side == 1 else bits - 1 - step))
            pairs.append((2 * h + (side ^ parity(h, bits)), 2 * to + (side ^ parity(to, bits))))
    return lax.ppermute(x, ("hub", "rep"), pairs)


def swap_blk(x, peers, step):
    pairs = []
    for z in range(peers):
        for c in range(2):
            to = z ^ (1 << (step if c == 1 else bits_of(peers) - 1 - step))
            pairs.append((2 * z + c, 2 * to + c))
    return lax.ppermute(x, ("blk", "rep"), pairs)


def on_device(
    source_feats,
    target_feats,
    hub_feats,
    weight_self,
    weight_neigh,
    bias_vector,
    send_rows,
    edge_target,
    edge_slot,
    hub_source,
    hub_target,
):
    shape = jax.ShapeDtypeStruct
    width = weight_neigh.shape[1]
    sizes = tuple(lax.axis_size(a) for a in ("blk", "hub", "rep"))
    peers, n_hub, n_rep = sizes
    assert n_rep == 2
    cap = send_rows.shape[2]
    per = hub_feats.shape[0]
    group_hubs = n_hub * n_rep * per
    assert group_hubs <= width
    slots = peers * cap + group_hubs
    targets = target_feats.shape[0]
    bias = bias_vector[None, :]

    half = group_hubs // 2
    outgoing, message, keep, cnt, e_tgt, e_slot, bias, hubs, tgt, w_self = call(
        functools.partial(project_kernel, sizes),
        (
            shape((peers * cap, width), BF16),
            shape((2 * half + COUNT_ROWS + per, width), BF16),
            shape((half, width), F32),
            shape((8, width), F32),
            shape(edge_target.shape, jnp.int32),
            shape(edge_slot.shape, jnp.int32),
            shape(bias.shape, F32),
            shape(hub_feats.shape, BF16),
            shape(target_feats.shape, BF16),
            shape(weight_self.shape, BF16),
        ),
        source_feats, hub_feats, weight_neigh, send_rows, hub_source, hub_target,
        edge_target, edge_slot, bias, target_feats, weight_self,
        hbm=True,
        scratch=[
            pltpu.VMEM(a.shape, a.dtype)
            for a in (source_feats, weight_neigh, send_rows, hub_source, hub_target)
        ]
        + [
            pltpu.VMEM((peers * cap + 2 * group_hubs, source_feats.shape[0]), BF16),
            pltpu.SemaphoreType.DMA((11,)),
        ],
    )

    got = lax.ppermute(message, "rep", [(i, i ^ 1) for i in range(n_rep)])
    for i in range(bits_of(n_hub)):
        half = keep.shape[0] // 2
        rows = got.shape[0] - 2 * keep.shape[0] - COUNT_ROWS
        message, keep, cnt = call(
            merge_kernel,
            (
                shape((2 * half + COUNT_ROWS + 2 * rows, width), BF16),
                shape((half, width), F32),
                shape((8, width), F32),
            ),
            got, message, keep, cnt,
        )
        got = swap_hub(message, n_hub, i)

    blocks = [outgoing[k * cap : (k + 1) * cap] for k in range(peers)]
    for i in range(bits_of(peers)):
        moved = [k for k in range(peers) if k >> i & 1]
        arrived = swap_blk(jnp.concatenate([blocks[k] for k in moved], axis=0), peers, i)
        for j, k in enumerate(moved):
            blocks[k] = arrived[j * cap : (j + 1) * cap]

    own, acc = call(
        functools.partial(own_kernel, sizes, cap, per),
        (shape((targets, width), F32), shape((targets, slots), F32)),
        tgt, w_self, bias, e_tgt, e_slot, mib=24,
    )
    late_rows = group_hubs // 2
    hi, lo, late, scale = call(
        functools.partial(count_kernel, sizes, cap, per),
        (
            shape((targets, slots - late_rows), BF16),
            shape((targets, slots - late_rows), BF16),
            shape((targets, 2 * late_rows), BF16),
            shape((targets, width), F32),
        ),
        acc, e_tgt, e_slot, mib=24,
    )
    mean, mine = call(
        blend_kernel,
        (shape((targets, width), F32), shape((per, width), F32)),
        hi, lo, own, scale, jnp.concatenate(blocks, axis=0), message, hubs, w_self, bias,
        mib=24 if slots > 1024 else 8,
        scratch=[pltpu.VMEM((slots - late_rows, width), BF16)],
    )
    return call(
        functools.partial(finish_kernel, sizes),
        (shape((targets, width), BF16), shape((per, width), BF16)),
        mean, late, scale, got, keep, cnt, mine,
    )


def solution(mesh):
    split = P(("blk", "hub", "rep"))

    return jax.shard_map(
        on_device,
        mesh=mesh,
        in_specs=(split,) * 3 + (P(),) * 3 + (split,) * 5,
        out_specs=(split, split),
        check_vma=False,
    )
```

```python
import functools

import jax
import jax.numpy as jnp
from jax import lax
from jax.experimental import pallas as pl
from jax.experimental.pallas import tpu as pltpu
from jax.sharding import PartitionSpec as P


F32 = jnp.float32
BF16 = jnp.bfloat16
COUNT_ROWS = 16
BASE = 256


def bits_of(size):
    bits = size.bit_length() - 1
    assert size == 1 << bits
    return bits


def one_hot(ids, rows):
    row = lax.broadcasted_iota(jnp.int32, (rows, ids.shape[1]), 0)
    return jnp.where(row == ids, 1.0, 0.0).astype(BF16)


def dot_nn(a, b):
    return jnp.dot(a, b, preferred_element_type=F32)


def dot_nt(a, b):
    return lax.dot_general(a, b, (((1,), (1,)), ((), ())), preferred_element_type=F32)


def split_count(x):
    high = jnp.floor(x * (1.0 / BASE))
    return high.astype(BF16), (x - BASE * high).astype(BF16)


def split_sum(x):
    high = x.astype(BF16)
    return high, (x - high.astype(F32)).astype(BF16)


def parity(value, bits):
    out = value & 1
    for i in range(1, bits):
        out = out ^ ((value >> i) & 1)
    return out


def places():
    return lax.axis_index("blk"), lax.axis_index("hub"), lax.axis_index("rep")


def crossed(x, bits):
    odd = parity(x, bits)
    return jnp.where(x == 0, 0, 1 - odd) if isinstance(x, jax.Array) else int(x != 0) & (1 - odd)


def project_kernel(
    sizes, src_h, hub_h, w_h, send_h, hs_h, ht_h, et_h, es_h, bias_h, tgt_h, ws_h,
    out, message, keep, cnt, et, es, bias, hub, tgt, ws,
    src, w, send, hs, ht, lhs, sem,
):
    peers, n_hub, n_rep = sizes
    z, h, c = places()
    copies = [
        pltpu.make_async_copy(a, b, sem.at[i])
        for i, (a, b) in enumerate(
            (
                (send_h, send), (hs_h, hs), (ht_h, ht),
                (src_h, src), (w_h, w), (hub_h, hub), (et_h, et), (es_h, es),
                (bias_h, bias), (ws_h, ws), (tgt_h, tgt),
            )
        )
    ]
    for copy in copies:
        copy.start()
    sources = src.shape[0]
    cap = send.shape[2]
    per = hub.shape[0]
    width = w.shape[1]
    total = n_hub * n_rep * per
    half = total // 2
    for copy in copies[:3]:
        copy.wait()
    for p in range(peers):
        row = send[0, pl.ds(p ^ z, 1), :]
        lhs[p * cap : (p + 1) * cap, :] = one_hot(row, sources).T
    target = ht[...]
    owner = target >> bits_of(per)
    x = (owner >> 1) ^ h
    order = x | (((owner & 1) ^ c ^ crossed(x, bits_of(n_hub))) << bits_of(n_hub))
    slot = (order << bits_of(per)) | (target & (per - 1))
    picks = one_hot(hs[...], sources)
    high, low = split_count(dot_nt(one_hot(slot, total), picks))
    base = peers * cap
    lhs[base : base + total, :] = low
    lhs[base + total :, :] = high
    ones = jnp.ones((8, target.shape[1]), BF16)
    counts = dot_nt(ones, one_hot(target, width))
    cnt[...] = counts
    high, low = split_count(counts)
    message[2 * half : 2 * half + COUNT_ROWS, :] = jnp.concatenate([high, low], axis=0)
    for copy in copies[3:6]:
        copy.wait()
    proj = dot_nn(src[...], w[...]).astype(BF16)
    message[2 * half + COUNT_ROWS :, :] = dot_nn(hub[...], w[...]).astype(BF16)
    got = dot_nn(lhs[...], proj)
    out[...] = got[:base].astype(BF16)
    sums = got[base : base + total] + BASE * got[base + total :]
    keep[...] = sums[:half]
    high, low = split_sum(sums[half:])
    message[:half, :] = high
    message[half : 2 * half, :] = low
    for copy in copies[6:]:
        copy.wait()


def merge_kernel(got, sent, kept, cnt, mine, new_cnt, hubs, *messages):
    n = kept.shape[0]
    per = mine.shape[0]
    sums = kept[...] + (got[:n].astype(F32) + got[n : 2 * n].astype(F32))
    mine[...] = sums[:per]
    high = got[2 * n : 2 * n + COUNT_ROWS].astype(F32)
    counts = cnt[...] + (BASE * high[:8] + high[8:])
    new_cnt[...] = counts
    rows = jnp.concatenate([sent[2 * n + COUNT_ROWS :, :], got[2 * n + COUNT_ROWS :, :]], axis=0)
    hubs[...] = rows
    shared = jnp.concatenate([*split_count(counts), rows], axis=0)
    for i, message in enumerate(messages):
        high, low = split_sum(sums[(i + 1) * per : (i + 2) * per])
        message[:per, :] = high
        message[per : 2 * per, :] = low
        message[2 * per :, :] = shared


def edge_slots(sizes, cap, per, raw):
    peers, n_hub, _ = sizes
    z, h, c = places()
    base = peers * cap
    low_slot = ((((raw >> bits_of(cap)) ^ z) << bits_of(cap)) | (raw & (cap - 1))) + (
        (2 * n_hub) * per
    )
    hub = raw - base
    owner = hub >> bits_of(per)
    x = (owner >> 1) ^ h
    q = (x << 1) | ((owner & 1) ^ c ^ crossed(x, bits_of(n_hub)))
    hub_slot = (q << bits_of(per)) | (hub & (per - 1))
    return jnp.where(raw < base, low_slot, hub_slot)


def edge_counts(targets, slots, target, slot, first, last):
    chunk = 512
    acc = jnp.zeros((targets, slots), F32)
    for s in range(first, last, chunk):
        acc = acc + dot_nt(
            one_hot(target[:, s : s + chunk], targets), one_hot(slot[:, s : s + chunk], slots)
        )
    return acc


def count_kernel(sizes, cap, per, tgt_feats, w, bias, e_tgt, e_slot, own, hi, lo, late, scale):
    own[...] = dot_nn(tgt_feats[...], w[...]) + bias[...]
    slot = edge_slots(sizes, cap, per, e_slot[...])
    slots = hi.shape[1] + late.shape[1] // 2
    counts = edge_counts(own.shape[0], slots, e_tgt[...], slot, 0, e_slot.shape[1])
    early = hi.shape[1]
    high = jnp.floor(counts * (1.0 / BASE))
    low = counts - BASE * high
    hi[...] = high[:, :early].astype(BF16)
    lo[...] = low[:, :early].astype(BF16)
    span = late.shape[1]
    lane = lax.broadcasted_iota(jnp.int32, late.shape, 1)
    moved = pltpu.roll(low[:, -span:], span // 2, 1)
    late[...] = jnp.where(lane < span // 2, moved, high[:, -span:]).astype(BF16)
    degree = jnp.maximum(jnp.sum(counts, axis=1, keepdims=True), 1.0)
    scale[...] = jnp.broadcast_to(1.0 / degree, scale.shape)


def blend_kernel(
    sizes, hi, lo, own, scale, rows, hubs, kept, cnt, hub, w, bias, *rest
):
    _, n_hub, n_rep = sizes
    _, h, c = places()
    *gots, mean, hub_mean, table = rest
    per = hub.shape[0]
    pair = 2 * per
    table[:pair, :] = hubs[...]
    sums = kept[...]
    counts = cnt[...]
    for i, got in enumerate(gots):
        table[(i + 1) * pair : (i + 2) * pair, :] = got[pair + COUNT_ROWS :, :]
        sums = sums + (got[:per].astype(F32) + got[per:pair].astype(F32))
        high = got[pair : pair + COUNT_ROWS].astype(F32)
        counts = counts + (BASE * high[:8] + high[8:])
    table[n_hub * pair :, :] = rows[...]
    values = table[...]
    neigh = BASE * dot_nn(hi[...], values) + dot_nn(lo[...], values)
    mean[...] = own[...] + neigh * scale[...]
    width = cnt.shape[1]
    row = lax.broadcasted_iota(jnp.int32, (per, width), 0)
    lane = lax.broadcasted_iota(jnp.int32, (per, width), 1)
    first = (h * n_rep + c) * per
    degree = jnp.sum(jnp.where(lane == row + first, counts[0:1, :], 0.0), axis=1, keepdims=True)
    result = dot_nn(hub[...], w[...]) + sums / jnp.maximum(degree, 1.0) + bias[...]
    hub_mean[...] = jnp.maximum(result, 0.0).astype(BF16)


def finish_kernel(mean, late, scale, rows, hub_mean, out, hub_out):
    values = rows[...]
    values = jnp.concatenate([values, (BASE * values.astype(F32)).astype(BF16)], axis=0)
    neigh = dot_nn(late[...], values)
    out[...] = jnp.maximum(mean[...] + neigh * scale[...], 0.0).astype(BF16)
    hub_out[...] = hub_mean[...]


def call(kernel, out_shape, *args, mib=8, hbm=False, scratch=()):
    spec = pl.BlockSpec(memory_space=pltpu.HBM if hbm else pltpu.VMEM)
    if hbm:
        args = [pltpu.with_memory_space_constraint(a, pltpu.HBM) for a in args]
    return pl.pallas_call(
        kernel,
        out_shape=out_shape,
        in_specs=[spec] * len(args),
        out_specs=jax.tree.map(lambda _: pl.BlockSpec(memory_space=pltpu.VMEM), out_shape),
        scratch_shapes=scratch,
        compiler_params=pltpu.CompilerParams(vmem_limit_bytes=mib << 20),
    )(*args)


def swap_hub(x, n_hub, bits):
    flip = crossed(bits, bits_of(n_hub))
    pairs = [(2 * h + c, 2 * (h ^ bits) + (c ^ flip)) for h in range(n_hub) for c in range(2)]
    return lax.ppermute(x, ("hub", "rep"), pairs)


def swap_blk(x, peers, step):
    return lax.ppermute(x, "blk", [(z, z ^ (1 << step)) for z in range(peers)])


def on_device(
    source_feats,
    target_feats,
    hub_feats,
    weight_self,
    weight_neigh,
    bias_vector,
    send_rows,
    edge_target,
    edge_slot,
    hub_source,
    hub_target,
):
    shape = jax.ShapeDtypeStruct
    width = weight_neigh.shape[1]
    sizes = tuple(lax.axis_size(a) for a in ("blk", "hub", "rep"))
    peers, n_hub, n_rep = sizes
    assert n_rep == 2
    cap = send_rows.shape[2]
    per = hub_feats.shape[0]
    group_hubs = n_hub * n_rep * per
    assert group_hubs <= width
    slots = peers * cap + group_hubs
    targets = target_feats.shape[0]
    bias = bias_vector[None, :]

    half = group_hubs // 2
    outgoing, message, keep, cnt, e_tgt, e_slot, bias, hubs, tgt, w_self = call(
        functools.partial(project_kernel, sizes),
        (
            shape((peers * cap, width), BF16),
            shape((2 * half + COUNT_ROWS + per, width), BF16),
            shape((half, width), F32),
            shape((8, width), F32),
            shape(edge_target.shape, jnp.int32),
            shape(edge_slot.shape, jnp.int32),
            shape(bias.shape, F32),
            shape(hub_feats.shape, BF16),
            shape(target_feats.shape, BF16),
            shape(weight_self.shape, BF16),
        ),
        source_feats, hub_feats, weight_neigh, send_rows, hub_source, hub_target,
        edge_target, edge_slot, bias, target_feats, weight_self,
        hbm=True,
        scratch=[
            pltpu.VMEM(a.shape, a.dtype)
            for a in (source_feats, weight_neigh, send_rows, hub_source, hub_target)
        ]
        + [
            pltpu.VMEM((peers * cap + 2 * group_hubs, source_feats.shape[0]), BF16),
            pltpu.SemaphoreType.DMA((11,)),
        ],
    )

    got = lax.ppermute(message, "rep", [(i, i ^ 1) for i in range(n_rep)])
    wide = shape((4 * per + COUNT_ROWS, width), BF16)
    keep, cnt, pair, *messages = call(
        merge_kernel,
        (
            shape((per, width), F32),
            shape((8, width), F32),
            shape((2 * per, width), BF16),
            *[wide] * (n_hub - 1),
        ),
        got, message, keep, cnt,
    )
    gots = [swap_hub(m, n_hub, i + 1) for i, m in enumerate(messages)]

    blocks = [outgoing[k * cap : (k + 1) * cap] for k in range(peers)]
    for i in range(bits_of(peers)):
        moved = [k for k in range(peers) if k >> i & 1]
        arrived = swap_blk(jnp.concatenate([blocks[k] for k in moved], axis=0), peers, i)
        for j, k in enumerate(moved):
            blocks[k] = arrived[j * cap : (j + 1) * cap]

    late_rows = peers * cap // 2
    own, hi, lo, late, scale = call(
        functools.partial(count_kernel, sizes, cap, per),
        (
            shape((targets, width), F32),
            shape((targets, slots - late_rows), BF16),
            shape((targets, slots - late_rows), BF16),
            shape((targets, 2 * late_rows), BF16),
            shape((targets, width), F32),
        ),
        tgt, w_self, bias, e_tgt, e_slot,
        mib=24,
    )
    mean, hub_mean = call(
        functools.partial(blend_kernel, sizes),
        (shape((targets, width), F32), shape((per, width), BF16)),
        hi, lo, own, scale, jnp.concatenate(blocks[: peers // 2], axis=0), pair, keep, cnt,
        hubs, w_self, bias, *gots,
        mib=24 if slots > 1024 else 8,
        scratch=[pltpu.VMEM((slots - late_rows, width), BF16)],
    )
    return call(
        finish_kernel,
        (shape((targets, width), BF16), shape((per, width), BF16)),
        mean, late, scale, arrived, hub_mean,
        mib=24 if slots > 1024 else 8,
    )


def solution(mesh):
    split = P(("blk", "hub", "rep"))

    return jax.shard_map(
        on_device,
        mesh=mesh,
        in_specs=(split,) * 3 + (P(),) * 3 + (split,) * 5,
        out_specs=(split, split),
        check_vma=False,
    )
```
